32 devices in a mesh: sec: 4 (over z), harm: 8 (over y, x, core).
Axes of the slice: x: 2, y: 2, z: 4, core: 2. Of those that a mesh axis runs over, the one named last changes fastest.
Arguments:
- displacement: bfloat16 [12, 64, 32, 48, 128], P('sec', 'harm'), may hold values from -3 to 3
- stiffness: bfloat16 [32, 1536, 1536], P('harm'), may hold values from -0.15625 to 0.15625
- contact_limit: float32 [12, 32, 48], P('sec', None, 'harm'), may hold values from 1 to 12
- pair_list: int32 [72, 3], replicated, may hold values from 0 to 31, as said below
- pair_count: int32 [4], replicated, may hold values from 3 to 18, as said below
Outputs:
- residual: bfloat16 [12, 64, 32, 48, 128], P('sec', 'harm')
The draws below stay inside these ranges and needn't reach their ends.
Inputs may be any that keep to these rules, and one draw needn't show every extreme that they name: `pair_list`: rows of index i of sec (the aligned blocks of 18 rows) have owners among sectors i * 3 to i * 3 + 2 and partners equal to owner + 1 or owner - 1 modulo 12; rows at or past that index's pair_count are unused and hold entries in range; among used rows of one index, at most 6 have partners on the same index, at most 6 on index i + 1 and at most 6 on index i - 1 (modulo the size of sec), and some index reaches 6 in all three groups in every draw. `pair_count`: every index of sec has at least one used row in each of its three groups; some index uses all its rows.
All inputs are finite; a program needn't handle non-finite values.
Results may differ from the reference program's by a relative error of at most 0.004.
Values may be sent and summed in bfloat16 or wider, within the bound.
No kernel may reach another device: no remote copies, remote signals or barrier semaphores. Data moves between devices by JAX's collectives and lax.ppermute only.
A program may use at most 192 MiB of HBM per device.

```python
import math
import jax
import jax.numpy as jnp
from jax import lax

H = 32
NT = 128
NBLK = 32
DPB = 48
SEC_DEV = 3
CAP = 6
BATCH = 128
NC = 64
IF = 1536
SECTORS = 12
PAIR_SLOTS = 18


def shuffled(seed_key):
    return jax.random.permutation(seed_key, PAIR_SLOTS)


def pair_tables(key):
    device_count = SECTORS // SEC_DEV
    subkeys = jax.random.split(jax.random.fold_in(key, 11), 6)
    load_table = jax.random.randint(subkeys[0], (device_count, 3), 1, CAP + 1)
    busiest = jax.random.randint(subkeys[1], (), 0, device_count)
    devices = jnp.arange(device_count, dtype=jnp.int32)[:, None]
    load_table = jnp.where(devices == busiest, CAP, load_table)
    slot_ids = jnp.arange(PAIR_SLOTS, dtype=jnp.int32)
    group = slot_ids // CAP
    filled = (slot_ids % CAP)[None, :] < load_table[:, group]
    shuffle = jax.vmap(shuffled)(jax.random.split(subkeys[2], device_count))
    scores = jnp.where(filled, 0, PAIR_SLOTS) + shuffle
    ordering = jnp.argsort(scores, axis=1, stable=True)
    group_sorted = jnp.take_along_axis(jnp.broadcast_to(group, (device_count, PAIR_SLOTS)), ordering, axis=1)
    owner_rand = jax.random.randint(subkeys[3], (device_count, PAIR_SLOTS), 0, SEC_DEV)
    step_sign = jax.random.randint(subkeys[4], (device_count, PAIR_SLOTS), 0, 2) * 2 - 1
    blocks = jax.random.randint(subkeys[5], (device_count, PAIR_SLOTS), 0, NBLK)
    inside = owner_rand + step_sign
    inside = jnp.where((inside < 0) | (inside >= SEC_DEV), owner_rand - step_sign, inside)
    local_owner = jnp.where(group_sorted == 0, owner_rand, jnp.where(group_sorted == 1, SEC_DEV - 1, 0))
    next_first = (devices + 1) % device_count * SEC_DEV
    prev_last = (devices + device_count - 1) % device_count * SEC_DEV + SEC_DEV - 1
    partner_global = jnp.where(group_sorted == 0, devices * SEC_DEV + inside, jnp.where(group_sorted == 1, next_first, prev_last))
    pair_rows = jnp.stack([devices * SEC_DEV + local_owner, partner_global, blocks], axis=2)
    counts = jnp.sum(load_table, axis=1)
    return (pair_rows.reshape(device_count * PAIR_SLOTS, 3).astype(jnp.int32), counts.astype(jnp.int32))


def draw_pair_list(key, part):
    return pair_tables(key)[0]


def draw_pair_count(key, part):
    return pair_tables(key)[1]


def block_scale(key, dims, pieces, smallest, top_value):
    def one(dim, blocks):
        steps = jax.random.uniform(jax.random.fold_in(jax.random.fold_in(key, 6), dim), (blocks,), jnp.float32, smallest / len(pieces), top_value / len(pieces))
        return jnp.repeat(jnp.exp(steps), dims[dim] // blocks).reshape((-1,) + (1,) * (len(dims) - dim - 1))

    level = one(*pieces[0])
    for cut in pieces[1:]:
        level = level * one(*cut)
    return level


def scatter_about(stream_key, extent, scale, limit, pieces=(), kind=jnp.bfloat16):
    values = jax.random.normal(stream_key, extent, jnp.float32) * scale
    if len(pieces) > 0:
        values = block_scale(stream_key, extent, pieces, -0.22, 0.18) * values
    return jnp.clip(values, min=-limit, max=limit).astype(kind)


def setup_inputs(seed: int = 0) -> dict:
    keys = jax.random.split(jax.random.key(seed), 6)
    return {
        "displacement": scatter_about(keys[0], (SECTORS, NC, NBLK, DPB, BATCH), 0.5, 3.0, ((0, 4), (1, 8))),
        "stiffness": scatter_about(keys[1], (H, IF, IF), IF ** -0.5, 0.15625, ((0, 8),)),
        "contact_limit": jnp.clip(jnp.exp(math.log(12.0) - 2.4849066 * jax.random.uniform(keys[2], (SECTORS, NBLK, DPB), jnp.float32) ** block_scale(keys[2], (SECTORS, NBLK, DPB), ((0, 4), (2, 8)), -0.2, 0.2)), 1.0, 12.0),
        "pair_list": draw_pair_list(jax.random.fold_in(keys[5], 71), 0),
        "pair_count": draw_pair_count(jax.random.fold_in(keys[5], 71), 0),
    }


def tables():
    n_index = jnp.arange(NT, dtype=jnp.int32)[:, None]
    c_index = jnp.arange(NC, dtype=jnp.int32)[None, :]
    harmonic = c_index // 2 + 1
    phases = ((harmonic * n_index) % NT).astype(jnp.float32) * (2.0 * math.pi / NT)
    waveform = jnp.where(c_index % 2 == 0, jnp.cos(phases), jnp.sin(phases))
    return waveform.astype(jnp.bfloat16), (waveform * (2.0 / NT)).astype(jnp.bfloat16)


def reference(displacement, stiffness, contact_limit, pair_list, pair_count):
    forward_table, inverse_table = tables()
    row_index = jnp.arange(pair_list.shape[0], dtype=jnp.int32)
    is_valid = (row_index % PAIR_SLOTS) < pair_count[row_index // PAIR_SLOTS]
    owners = pair_list[:, 0]
    partners = pair_list[:, 1]
    blocks = pair_list[:, 2]
    by_dof = jnp.moveaxis(displacement, 3, 0)
    limit_dof = jnp.moveaxis(contact_limit, 2, 0)

    def one_dof(inputs):
        coeff_slab, limit_slab = inputs
        samples = jnp.einsum('nc,scbx->snbx', forward_table.astype(jnp.float32), coeff_slab.astype(jnp.float32),
                             precision=lax.Precision.HIGHEST).astype(jnp.bfloat16)
        relative = samples[owners, :, blocks].astype(jnp.float32) - samples[partners, :, blocks].astype(jnp.float32)
        limits = limit_slab[partners, blocks][:, None, None]
        friction = jnp.where(is_valid[:, None, None], limits * jnp.tanh(relative / limits), jnp.float32(0.0))
        friction = lax.optimization_barrier(friction.astype(jnp.bfloat16)).astype(jnp.float32)
        pair_coeffs = jnp.einsum('nc,rnx->rcx', inverse_table.astype(jnp.float32), friction,
                                 precision=lax.Precision.HIGHEST)
        pair_coeffs = lax.optimization_barrier(pair_coeffs.astype(jnp.bfloat16)).astype(jnp.float32)
        force = jnp.zeros((SECTORS, NC, NBLK, BATCH), jnp.float32)
        force = force.at[owners, :, blocks].add(pair_coeffs)
        force = force.at[partners, :, blocks].add(-pair_coeffs)
        return force.astype(jnp.bfloat16)

    force_slabs = lax.map(one_dof, (by_dof, limit_dof))
    force_coeffs = jnp.moveaxis(force_slabs, 0, 3)
    paired = jnp.moveaxis(displacement.reshape(SECTORS, H, 2, IF, BATCH), 1, 0)
    paired_force = jnp.moveaxis(force_coeffs.reshape(SECTORS, H, 2, IF, BATCH), 1, 0)

    def one_harmonic(inputs):
        matrix, coeff_slab, force_slab = inputs
        elastic = jnp.einsum('ij,spjx->spix', matrix.astype(jnp.float32), coeff_slab.astype(jnp.float32),
                             precision=lax.Precision.HIGHEST)
        return (elastic + force_slab.astype(jnp.float32)).astype(jnp.bfloat16)

    stacked = lax.map(one_harmonic, (stiffness, paired, paired_force))
    return jnp.moveaxis(stacked, 0, 1).reshape(SECTORS, NC, NBLK, DPB, BATCH)
```

```python
import functools
import math

import jax
import jax.numpy as jnp
import numpy as np
from jax import lax
from jax.experimental import pallas as pl
from jax.experimental.pallas import tpu as pltpu
from jax.sharding import PartitionSpec as P

NT = 128
ANY = pl.BlockSpec(memory_space=pl.ANY)
SMEM = pl.BlockSpec(memory_space=pltpu.SMEM)
VMEM = pl.BlockSpec(memory_space=pltpu.VMEM)
F32 = jnp.float32
BF16 = jnp.bfloat16


def tables(sample_count, coeff_count):
    n_index = jnp.arange(sample_count, dtype=jnp.int32)[:, None]
    c_index = jnp.arange(coeff_count, dtype=jnp.int32)[None, :]
    harmonic = c_index // 2 + 1
    phases = (harmonic * n_index % sample_count).astype(F32) * (2.0 * math.pi / sample_count)
    waveform = jnp.where(c_index % 2 == 0, jnp.cos(phases), jnp.sin(phases))
    return waveform.astype(BF16), (waveform * (2.0 / sample_count)).astype(BF16)


def swap_matrix(coeffs, dofs):
    size = coeffs * dofs
    out = np.zeros((size, size), np.float32)
    d, c = np.meshgrid(np.arange(dofs), np.arange(coeffs), indexing="ij")
    out[(d * coeffs + c).ravel(), (c * dofs + d).ravel()] = 1.0
    return out


def build_table(cap, sectors_here, sec_count, sec_ref, list_ref, count_ref, tab_ref):
    slots = 3 * cap
    me = sec_ref[0]
    total = sectors_here * sec_count

    def clear(i, carry):
        tab_ref[i] = 0
        return carry

    lax.fori_loop(0, 6 * slots, clear, 0)

    def scan(device, emit):
        used = count_ref[device]

        def row(r, ranks):
            at = device * slots + r
            owner, partner, block = list_ref[0, at], list_ref[1, at], list_ref[2, at]
            local = partner - device * sectors_here
            here = (local >= 0) & (local < sectors_here)
            following = jnp.where(owner + 1 == total, 0, owner + 1)
            group = jnp.where(here, 0, jnp.where(partner == following, 1, 2))
            valid = r < used
            rank = jnp.where(group == 0, ranks[0], jnp.where(group == 1, ranks[1], ranks[2]))

            @pl.when(valid & (rank < cap))
            def _():
                emit(group, rank, owner, partner, block)

            return tuple(
                ranks[g] + jnp.where(valid & (group == g), 1, 0).astype(jnp.int32)
                for g in range(3)
            )

        lax.fori_loop(0, slots, row, (jnp.int32(0),) * 3)

    base = me * sectors_here

    def own(group, rank, owner, partner, block):
        at = group * cap + rank
        tab_ref[3 * slots + at] = owner - base
        tab_ref[4 * slots + at] = block
        tab_ref[5 * slots + at] = 1

        @pl.when(group == 0)
        def _():
            tab_ref[at] = partner - base
            tab_ref[slots + at] = block
            tab_ref[2 * slots + at] = 1

    def incoming(wanted):
        def emit(group, rank, owner, partner, block):
            @pl.when(group == wanted)
            def _():
                at = wanted * cap + rank
                tab_ref[at] = partner - base
                tab_ref[slots + at] = block
                tab_ref[2 * slots + at] = 1

        return emit

    scan(me, own)
    scan(jnp.where(me == 0, sec_count - 1, me - 1), incoming(1))
    scan(jnp.where(me == sec_count - 1, 0, me + 1), incoming(2))


def fetch(disp_ref, tab_ref, sec_at, blk_at, buf, sem):
    return pltpu.make_async_copy(disp_ref.at[tab_ref[sec_at], :, tab_ref[blk_at]], buf, sem)


def swapped(perm_ref, value):
    rows = value.shape[0] * value.shape[1]
    return jnp.dot(perm_ref[...], value.reshape(rows, value.shape[2]), preferred_element_type=F32)


def send_kernel(cap, sectors_here, sec_count, sec_ref, list_ref, count_ref, perm_ref, disp_ref,
                next_ref, prev_ref, tab_ref, raw, sem):
    slots = 3 * cap
    build_table(cap, sectors_here, sec_count, sec_ref, list_ref, count_ref, tab_ref)
    copies = [
        fetch(disp_ref, tab_ref, 3 * slots + cap + k, 4 * slots + cap + k, raw.at[k], sem.at[k])
        for k in range(2 * cap)
    ]
    for copy in copies:
        copy.start()
    peers, rows = next_ref.shape[0], next_ref.shape[2]
    for k in range(2 * cap):
        copies[k].wait()
        value = swapped(perm_ref, raw[k]).astype(BF16)
        for h in range(peers):
            target = next_ref if k < cap else prev_ref
            target[h, k % cap] = value[h * rows : (h + 1) * rows]


def local_kernel(cap, tab_ref, perm_ref, disp_ref, diff_ref, a_ref, b_ref, raw, sem):
    slots = 3 * cap
    copies = [
        fetch(disp_ref, tab_ref, 3 * slots + k, 4 * slots + k, raw.at[k], sem.at[k])
        for k in range(cap)
    ] + [
        fetch(disp_ref, tab_ref, k, slots + k, raw.at[cap + k], sem.at[cap + k])
        for k in range(slots)
    ]
    for copy in copies:
        copy.start()
    peers, rows = diff_ref.shape[0], diff_ref.shape[2]
    for k in range(cap):
        copies[k].wait()
    for k in range(slots):
        copies[cap + k].wait()
        value = swapped(perm_ref, raw[cap + k])
        if k < cap:
            value = swapped(perm_ref, raw[k]) - value
        value = value.astype(BF16)
        target = (diff_ref, a_ref, b_ref)[k // cap]
        for h in range(peers):
            target[h, k % cap] = value[h * rows : (h + 1) * rows]


def friction_kernel(cap, group, blocks, tab_ref, lim_ref, rec_ref, fwd_ref, inv_ref, x_ref, o_ref):
    slots = 3 * cap
    peers, rows, lanes = x_ref.shape[0], x_ref.shape[2], x_ref.shape[3]
    coeffs = fwd_ref.shape[1] // peers
    dofs = rows // coeffs
    for k in range(cap):
        p = group * cap + k
        base = (tab_ref[p] * blocks + tab_ref[slots + p]) * dofs
        parts = [x_ref[h, k].astype(F32) for h in range(peers)]
        columns = jnp.concatenate(
            [
                jnp.concatenate([x[d * coeffs : (d + 1) * coeffs] for x in parts], axis=0)
                for d in range(dofs)
            ],
            axis=1,
        ).astype(BF16)
        wave = jnp.dot(fwd_ref[...], columns, preferred_element_type=F32)
        force = jnp.concatenate(
            [
                lim_ref[base + d] * jnp.tanh(wave[:, d * lanes : (d + 1) * lanes] * rec_ref[base + d])
                for d in range(dofs)
            ],
            axis=1,
        ).astype(BF16)
        back = jnp.dot(inv_ref[...], force, preferred_element_type=F32)
        for h in range(peers):
            o_ref[h, k] = jnp.concatenate(
                [
                    back[h * coeffs : (h + 1) * coeffs, d * lanes : (d + 1) * lanes]
                    for d in range(dofs)
                ],
                axis=0,
            ).astype(BF16)


def add_kernel(specs, keep, *refs):
    count = len({s[0] for s in specs})
    tab_ref, perm_ref = refs[0], refs[1]
    parts = refs[2 : 2 + count]
    prod_in, out_in = refs[2 + count : 4 + count]
    rest = refs[4 + count :]
    if keep:
        prod_ref, out_ref, acc, obuf, lead, sem_in, sem_out, sem_keep = rest
    else:
        out_ref, acc, obuf, lead, sem_in, sem_out = rest
        prod_ref = prod_in
    n = len(specs)

    for j, (_, _, sec_at, blk_at, live_at, _) in enumerate(specs):
        where = jnp.int32(j)
        for i in range(j - 1, -1, -1):
            _, _, s2, b2, l2, _ = specs[i]
            same = (
                (tab_ref[s2] == tab_ref[sec_at])
                & (tab_ref[b2] == tab_ref[blk_at])
                & (tab_ref[l2] > 0)
            )
            where = jnp.where(same, i, where)
        lead[j] = jnp.where(tab_ref[live_at] > 0, where, -1)

    def slot(ref, j):
        return ref.at[tab_ref[specs[j][2]], :, tab_ref[specs[j][3]]]

    def load(j):
        return pltpu.make_async_copy(slot(prod_ref, j), acc.at[j], sem_in.at[j])

    def store(j):
        return pltpu.make_async_copy(obuf.at[j], slot(out_ref, j), sem_out.at[j])

    def store_keep(j):
        return pltpu.make_async_copy(acc.at[j], slot(prod_ref, j), sem_keep.at[j])

    for j in range(n):
        pl.when(lead[j] == j)(lambda j=j: load(j).start())
    for j in range(n):
        pl.when(lead[j] == j)(lambda j=j: load(j).wait())
    for j, (part, k, _, _, _, sign) in enumerate(specs):

        @pl.when(lead[j] >= 0)
        def _(j=j, part=part, k=k, sign=sign):
            ref = parts[part]
            value = jnp.concatenate([ref[h, k] for h in range(ref.shape[0])], axis=0)
            term = jnp.dot(perm_ref[...], value, preferred_element_type=F32)
            term = term.reshape(acc.shape[1:])
            at = jnp.maximum(lead[j], 0)
            acc[at] = acc[at] + (term if sign > 0 else -term)

    for j in range(n):

        @pl.when(lead[j] == j)
        def _(j=j):
            obuf[j] = acc[j].astype(BF16)
            store(j).start()
            if keep:
                store_keep(j).start()

    for j in range(n):

        @pl.when(lead[j] == j)
        def _(j=j):
            store(j).wait()
            if keep:
                store_keep(j).wait()


def add_pairs(specs, keep, tab, perm_t, parts, prod, out):
    n = len(specs)
    slot_shape = (prod.shape[1], prod.shape[3], prod.shape[4])
    at = 2 + len(parts)
    scratch = [
        pltpu.VMEM((n,) + slot_shape, F32),
        pltpu.VMEM((n,) + slot_shape, BF16),
        pltpu.SMEM((n,), jnp.int32),
        pltpu.SemaphoreType.DMA((n,)),
        pltpu.SemaphoreType.DMA((n,)),
    ]
    out_shape = [jax.ShapeDtypeStruct(out.shape, out.dtype)]
    aliases = {at + 1: 0}
    if keep:
        scratch.append(pltpu.SemaphoreType.DMA((n,)))
        out_shape = [jax.ShapeDtypeStruct(prod.shape, prod.dtype)] + out_shape
        aliases = {at: 0, at + 1: 1}
    return pl.pallas_call(
        functools.partial(add_kernel, specs, keep),
        out_shape=out_shape,
        in_specs=[SMEM, VMEM] + [VMEM] * len(parts) + [ANY, ANY],
        out_specs=[ANY] * len(out_shape),
        scratch_shapes=scratch,
        input_output_aliases=aliases,
        name="add_pairs",
    )(tab, perm_t, *parts, prod, out)


def stiffness_kernel(matrix_ref, x_ref, prod_ref, out_ref):
    sectors = x_ref.shape[0]
    matrix = matrix_ref[0]
    lanes = x_ref.shape[4]
    for s in range(sectors):
        rhs = jnp.concatenate([x_ref[s, 0, 0], x_ref[s, 0, 1]], axis=1)
        value = jnp.dot(matrix, rhs, preferred_element_type=F32)
        for p in range(2):
            part = value[:, p * lanes : (p + 1) * lanes]
            prod_ref[s, 0, p] = part
            out_ref[s, 0, p] = part.astype(BF16)


def stiffness_product(stiffness, paired):
    harmonics, size, _ = stiffness.shape
    sectors, _, _, _, lanes = paired.shape
    tile = size // 2
    block = (sectors, 1, 2, tile, lanes)
    return pl.pallas_call(
        stiffness_kernel,
        grid=(harmonics, size // tile),
        in_specs=[
            pl.BlockSpec((1, tile, size), lambda i, j: (i, j, 0)),
            pl.BlockSpec((sectors, 1, 2, size, lanes), lambda i, j: (0, i, 0, 0, 0)),
        ],
        out_specs=[pl.BlockSpec(block, lambda i, j: (0, i, 0, j, 0))] * 2,
        out_shape=[
            jax.ShapeDtypeStruct(paired.shape, F32),
            jax.ShapeDtypeStruct(paired.shape, BF16),
        ],
        cost_estimate=pl.CostEstimate(
            flops=2 * harmonics * size * size * sectors * 2 * lanes,
            bytes_accessed=2 * stiffness.size + 8 * paired.size,
            transcendentals=0,
        ),
        name="stiffness_product",
    )(stiffness, paired)


def on_device(displacement, stiffness, contact_limit, pair_list, pair_count):
    sec_count = lax.axis_size("sec")
    harm_count = lax.axis_size("harm")
    sectors, coeffs, blocks, dofs, lanes = displacement.shape
    cap = pair_list.shape[0] // sec_count // 3
    slots = 3 * cap
    rows = coeffs * dofs // harm_count
    fwd, inv = tables(NT, coeffs * harm_count)
    inv = inv.T
    perm_np = swap_matrix(coeffs, dofs)
    perm, perm_t = jnp.asarray(perm_np, BF16), jnp.asarray(perm_np.T, BF16)
    wire = jax.ShapeDtypeStruct((harm_count, cap, rows, lanes), BF16)
    sec = lax.axis_index("sec").astype(jnp.int32).reshape(1)
    raw_slot = (coeffs, dofs, lanes)

    to_next, to_prev, tab = pl.pallas_call(
        functools.partial(send_kernel, cap, sectors, sec_count),
        out_shape=[wire, wire, jax.ShapeDtypeStruct((6 * slots,), jnp.int32)],
        in_specs=[SMEM, SMEM, SMEM, VMEM, ANY],
        out_specs=[VMEM, VMEM, SMEM],
        scratch_shapes=[
            pltpu.VMEM((2 * cap,) + raw_slot, BF16),
            pltpu.SemaphoreType.DMA((2 * cap,)),
        ],
        name="send",
    )(sec, pair_list.T, pair_count, perm, displacement)

    forward = [(i, (i + 1) % sec_count) for i in range(sec_count)]
    backward = [((i + 1) % sec_count, i) for i in range(sec_count)]
    from_prev = lax.ppermute(to_next, "sec", forward)
    from_next = lax.ppermute(to_prev, "sec", backward)

    diff_local, at_a, at_b = pl.pallas_call(
        functools.partial(local_kernel, cap),
        out_shape=[wire] * 3,
        in_specs=[SMEM, VMEM, ANY],
        out_specs=[VMEM] * 3,
        scratch_shapes=[
            pltpu.VMEM((4 * cap,) + raw_slot, BF16),
            pltpu.SemaphoreType.DMA((4 * cap,)),
        ],
        name="local",
    )(tab, perm, displacement)

    limit = contact_limit.reshape(-1)
    reciprocal = 1.0 / limit

    def exchange(x):
        return lax.all_to_all(x, "harm", split_axis=0, concat_axis=0, tiled=True)

    def friction(group, x):
        return pl.pallas_call(
            functools.partial(friction_kernel, cap, group, blocks),
            out_shape=wire,
            in_specs=[SMEM, SMEM, SMEM, VMEM, VMEM, VMEM],
            out_specs=VMEM,
            name="friction",
        )(tab, limit, reciprocal, fwd, inv, x)

    def difference(x, y):
        return (x.astype(F32) - y.astype(F32)).astype(BF16)

    local_x = exchange(diff_local)
    force_local = friction(0, local_x)
    a_x = exchange(difference(from_prev, at_a))
    force_a = friction(1, a_x)
    b_x = exchange(difference(from_next, at_b))
    force_b = friction(2, b_x)
    back_a = exchange(force_a)
    ret_a = lax.ppermute(back_a, "sec", backward)
    back_b = exchange(force_b)
    ret_b = lax.ppermute(back_b, "sec", forward)
    back_local = exchange(force_local)

    paired = displacement.reshape(sectors, coeffs // 2, 2, blocks * dofs, lanes)
    prod, out = stiffness_product(stiffness, paired)
    prod = prod.reshape(displacement.shape)
    out = out.reshape(displacement.shape)

    def partner(part, group):
        return [
            (part, k, g, slots + g, 2 * slots + g, -1)
            for k, g in enumerate(range(group * cap, (group + 1) * cap))
        ]

    def owner(part, group):
        return [
            (part, k, 3 * slots + g, 4 * slots + g, 5 * slots + g, 1)
            for k, g in enumerate(range(group * cap, (group + 1) * cap))
        ]

    prod, out = add_pairs(partner(0, 1), True, tab, perm_t, [back_a], prod, out)
    prod, out = add_pairs(partner(0, 2), True, tab, perm_t, [back_b], prod, out)
    prod, out = add_pairs(partner(0, 0) + owner(0, 0), True, tab, perm_t, [back_local], prod, out)
    (out,) = add_pairs(owner(0, 1) + owner(1, 2), False, tab, perm_t, [ret_a, ret_b], prod, out)
    return out


def solution(mesh):
    in_specs = (
        P("sec", "harm", None, None, None),
        P("harm", None, None),
        P("sec", None, "harm"),
        P(),
        P(),
    )
    out_specs = P("sec", "harm", None, None, None)
    return jax.shard_map(
        on_device, mesh=mesh, in_specs=in_specs, out_specs=out_specs, check_vma=False
    )
```

```python
import functools
import math

import jax
import jax.numpy as jnp
import numpy as np
from jax import lax
from jax.experimental import pallas as pl
from jax.experimental.pallas import tpu as pltpu
from jax.sharding import PartitionSpec as P


NT = 128
ANY = pl.BlockSpec(memory_space=pl.ANY)
SMEM = pl.BlockSpec(memory_space=pltpu.SMEM)
VMEM = pl.BlockSpec(memory_space=pltpu.VMEM)
F32 = jnp.float32
BF16 = jnp.bfloat16


def tables(sample_count, coeff_count):
    n_index = np.arange(sample_count)[:, None]
    c_index = np.arange(coeff_count)[None, :]
    phases = 2.0 * math.pi * ((c_index // 2 + 1) * n_index % sample_count) / sample_count
    wave = np.where(c_index % 2 == 0, np.cos(phases), np.sin(phases)).astype(np.float32)
    return jnp.asarray(wave, BF16), jnp.asarray(wave.T * np.float32(2.0 / sample_count), BF16)


def memory(mib):
    return pltpu.CompilerParams(vmem_limit_bytes=mib << 20)


def scan_rows(cap, sectors_here, sec_count, list_ref, count_ref, device, emit):
    slots = 3 * cap
    total = sectors_here * sec_count
    used = count_ref[device]

    def row(r, ranks):
        at = device * slots + r
        owner, partner, block = list_ref[0, at], list_ref[1, at], list_ref[2, at]
        local = partner - device * sectors_here
        here = (local >= 0) & (local < sectors_here)
        following = jnp.where(owner + 1 == total, 0, owner + 1)
        group = jnp.where(here, 0, jnp.where(partner == following, 1, 2))
        valid = r < used
        rank = jnp.where(group == 0, ranks[0], jnp.where(group == 1, ranks[1], ranks[2]))

        @pl.when(valid & (rank < cap))
        def _():
            emit(group, rank, owner, partner, block)

        return tuple(
            ranks[g] + jnp.where(valid & (group == g), 1, 0).astype(jnp.int32) for g in range(3)
        )

    lax.fori_loop(0, slots, row, (jnp.int32(0),) * 3)


def widen(value):
    return value.astype(F32).reshape(-1, value.shape[-1])


def unrolled(count):
    return next(u for u in (3, 2, 1) if count % u == 0)


def each(count, body):
    def step(k, carry):
        body(k)
        return carry

    lax.fori_loop(0, count, step, 0)


def batched(count, stage, process):
    width = unrolled(count)

    def step(i, carry):
        for u in range(width):
            stage(i * width + u, u)
        for u in range(width):
            process(i * width + u, u)
        return carry

    lax.fori_loop(0, count // width, step, 0)


def swap_rows(tmp_ref, buf, coeffs, dofs):
    peers, rows = buf.shape[0], buf.shape[1]
    share = rows // coeffs
    for h in range(peers):
        buf[h] = jnp.concatenate(
            [tmp_ref[pl.ds(h * share + d, coeffs, stride=dofs), :] for d in range(share)], axis=0
        ).astype(BF16)


def send_kernel(cap, sectors_here, sec_count, sec_ref, list_ref, count_ref, disp_ref,
                next_ref, prev_ref, own_ref, raw, buf, sem, sem_out, *tmp):
    slots = 3 * cap
    me = sec_ref[0]
    base = me * sectors_here

    def clear(i):
        own_ref[i] = 0

    each(4 * slots, clear)

    def own(group, rank, owner, partner, block):
        at = group * cap + rank
        own_ref[at] = owner - base
        own_ref[slots + at] = block
        own_ref[2 * slots + at] = 1
        own_ref[3 * slots + at] = partner - base

    scan_rows(cap, sectors_here, sec_count, list_ref, count_ref, me, own)

    def copy(k):
        at = cap + k
        source = disp_ref.at[own_ref[at], :, own_ref[slots + at]]
        return pltpu.make_async_copy(source, raw.at[k], sem.at[k])

    each(2 * cap, lambda k: copy(k).start())
    coeffs, dofs = raw.shape[1], raw.shape[2]

    def out(g, k):
        target = (next_ref, prev_ref)[g]
        return pltpu.make_async_copy(buf.at[g * cap + k], target.at[:, k], sem_out.at[g * cap + k])

    for g in range(2):

        def stage(k, u, g=g):
            copy(g * cap + k).wait()
            tmp[u][...] = widen(raw[g * cap + k])

        def process(k, u, g=g):
            swap_rows(tmp[u], buf.at[g * cap + k], coeffs, dofs)
            out(g, k).start()

        batched(cap, stage, process)
    for g in range(2):
        each(cap, lambda k, g=g: out(g, k).wait())


def find_leaders(cap, blocks, sectors_here, calls, tab_ref, lead_ref, seen):
    slots = 3 * cap
    start = 0
    for firsts in calls:

        def clear(i):
            seen[i] = -1

        each(sectors_here * blocks, clear)
        for i, first in enumerate(firsts):

            def mark(k, i=i, first=first, start=start):
                at = first + k
                j = i * cap + k
                key = tab_ref[at] * blocks + tab_ref[slots + at]
                live = tab_ref[2 * slots + at] > 0
                found = jnp.where(seen[key] < 0, j, seen[key])
                lead_ref[start + j] = jnp.where(live, found, -1)
                seen[key] = jnp.where(live, found, seen[key])

            each(cap, mark)
        start += cap * len(firsts)


def local_kernel(cap, own_ref, disp_ref, diff_ref, raw, buf, sem, sem_out, *tmp):
    slots = 3 * cap

    def copy(sec_at, blk_at, j):
        source = disp_ref.at[own_ref[sec_at], :, own_ref[blk_at]]
        return pltpu.make_async_copy(source, raw.at[j], sem.at[j])

    def owner(k):
        return copy(k, slots + k, k)

    def partner(k):
        return copy(3 * slots + k, slots + k, cap + k)

    def start(k):
        owner(k).start()
        partner(k).start()

    each(cap, start)
    coeffs, dofs = raw.shape[1], raw.shape[2]

    def out(k):
        return pltpu.make_async_copy(buf.at[k], diff_ref.at[:, k], sem_out.at[k])

    def stage(k, u):
        owner(k).wait()
        partner(k).wait()
        tmp[u][...] = widen(raw[k]) - widen(raw[cap + k])

    def process(k, u):
        swap_rows(tmp[u], buf.at[k], coeffs, dofs)
        out(k).start()

    batched(cap, stage, process)
    each(cap, lambda k: out(k).wait())


def partner_kernel(cap, sectors_here, sec_count, calls, sec_ref, list_ref, count_ref, own_ref,
                   lim_ref, disp_ref, dep_ref, a_ref, b_ref, tab_ref, lead_ref, pick_ref, raw,
                   buf, seen, sem, sem_out, *tmp):
    slots = 3 * cap
    me = sec_ref[0]
    base = me * sectors_here

    def fill(i):
        keep = lax.rem(i, slots) < cap
        tab_ref[3 * slots + i] = own_ref[i]
        first = jnp.where(i < slots, own_ref[3 * slots + lax.rem(i, slots)], own_ref[i])
        tab_ref[i] = jnp.where(keep, first, 0)

    each(3 * slots, fill)
    scan = functools.partial(scan_rows, cap, sectors_here, sec_count, list_ref, count_ref)

    def incoming(wanted):
        def emit(group, rank, owner, partner, block):
            @pl.when(group == wanted)
            def _():
                at = wanted * cap + rank
                tab_ref[at] = partner - base
                tab_ref[slots + at] = block
                tab_ref[2 * slots + at] = 1

        return emit

    scan(jnp.where(me == 0, sec_count - 1, me - 1), incoming(1))
    scan(jnp.where(me == sec_count - 1, 0, me + 1), incoming(2))

    def copy(j):
        source = disp_ref.at[tab_ref[cap + j], :, tab_ref[slots + cap + j]]
        return pltpu.make_async_copy(source, raw.at[j], sem.at[j])

    each(2 * cap, lambda j: copy(j).start())
    blocks = disp_ref.shape[2]
    find_leaders(cap, blocks, sectors_here, calls, tab_ref, lead_ref, seen)
    total = lim_ref.shape[0] // 2
    share = total // (sectors_here * blocks)

    def pick(p):
        at = (tab_ref[p] * blocks + tab_ref[slots + p]) * share
        for d in range(share):
            pick_ref[p * share + d] = lim_ref[at + d]
            pick_ref[(slots + p) * share + d] = lim_ref[total + at + d]

    each(slots, pick)
    coeffs, dofs = raw.shape[1], raw.shape[2]
    targets = (a_ref, b_ref)

    def out(g, k):
        j = g * cap + k
        return pltpu.make_async_copy(buf.at[j], targets[g].at[:, k], sem_out.at[j])

    for g in range(2):

        def stage(k, u, g=g):
            copy(g * cap + k).wait()
            tmp[u][...] = widen(raw[g * cap + k])

        def process(k, u, g=g):
            swap_rows(tmp[u], buf.at[g * cap + k], coeffs, dofs)
            out(g, k).start()

        batched(cap, stage, process)
    for g in range(2):
        each(cap, lambda k, g=g: out(g, k).wait())


def friction_pair(base, rec_base, lim_ref, fwd_ref, inv_ref, x_ref, o_ref):
    peers, rows, lanes = x_ref.shape
    coeffs = fwd_ref.shape[1] // peers
    dofs = rows // coeffs
    parts = [x_ref[h].astype(F32) for h in range(peers)]
    columns = jnp.concatenate(
        [
            jnp.concatenate([x[d * coeffs : (d + 1) * coeffs] for x in parts], axis=0)
            for d in range(dofs)
        ],
        axis=1,
    ).astype(BF16)
    wave = jnp.dot(fwd_ref[...], columns, preferred_element_type=F32)
    force = jnp.concatenate(
        [
            lim_ref[base + d]
            * jnp.tanh(wave[:, d * lanes : (d + 1) * lanes] * lim_ref[rec_base + d])
            for d in range(dofs)
        ],
        axis=1,
    ).astype(BF16)
    back = jnp.dot(inv_ref[...], force, preferred_element_type=F32)
    for h in range(peers):
        o_ref[h] = jnp.concatenate(
            [
                back[h * coeffs : (h + 1) * coeffs, d * lanes : (d + 1) * lanes]
                for d in range(dofs)
            ],
            axis=0,
        ).astype(BF16)


def difference_kernel(x_ref, y_ref, *refs):
    o_ref = refs[-1]

    def subtract(h):
        o_ref[h] = (x_ref[h].astype(F32) - y_ref[h].astype(F32)).astype(BF16)

    each(x_ref.shape[0], subtract)


def friction_kernel(cap, group, first, with_difference, lim_ref, fwd_ref, inv_ref, x_ref, *refs):
    slots = 3 * cap
    if with_difference:
        y_ref, z_ref, o_ref, x_buf, o_buf, sem, y_buf, z_buf = refs
    else:
        o_ref, x_buf, o_buf, sem = refs
    dofs = x_ref.shape[2] * x_ref.shape[0] // fwd_ref.shape[1]

    def load(k):
        return pltpu.make_async_copy(x_ref.at[:, first + k], x_buf.at[k], sem.at[0, k])

    def load_y(k):
        return pltpu.make_async_copy(y_ref.at[:, k], y_buf.at[k], sem.at[2, k])

    def load_z(k):
        return pltpu.make_async_copy(z_ref.at[:, k], z_buf.at[k], sem.at[3, k])

    def out(k):
        return pltpu.make_async_copy(o_buf.at[k], o_ref.at[:, k], sem.at[1, k])

    each(cap, lambda k: load(k).start())
    if with_difference:

        def start(k):
            load_y(k).start()
            load_z(k).start()

        each(cap, start)

    def stage(k, u):
        load(k).wait()

    def process(k, u):
        base = (group * cap + k) * dofs
        rec_base = base + slots * dofs
        friction_pair(base, rec_base, lim_ref, fwd_ref, inv_ref, x_buf.at[k], o_buf.at[k])
        out(k).start()

    batched(cap, stage, process)
    if with_difference:

        def subtract(k):
            load_y(k).wait()
            load_z(k).wait()
            o_buf[cap + k] = (y_buf[k].astype(F32) - z_buf[k].astype(F32)).astype(BF16)
            out(cap + k).start()

        each(cap, subtract)
        each(2 * cap, lambda k: out(k).wait())
    else:
        each(cap, lambda k: out(k).wait())


def add_kernel(cap, specs, start, n_deps, tab_ref, lead_ref, *refs):
    n_parts = len({spec[0] for spec in specs})
    parts = refs[:n_parts]
    refs = refs[n_parts + n_deps + 1 :]
    out_ref, acc, obuf, pbuf, sem_in, sem_part, sem_out = refs[:7]
    tmp = refs[7:]
    slots = 3 * cap
    coeffs, dofs = acc.shape[1], acc.shape[2]

    def slot(first, k):
        return out_ref.at[tab_ref[first + k], :, tab_ref[slots + first + k]]

    for i, (part, first_part, first, _) in enumerate(specs):

        def load(k, i=i, part=part, first_part=first_part, first=first):
            j = i * cap + k
            at = lead_ref[start + j]

            @pl.when(at >= 0)
            def _():
                pltpu.make_async_copy(
                    parts[part].at[:, first_part + k], pbuf.at[j], sem_part.at[j]
                ).start()

            @pl.when(at == j)
            def _():
                pltpu.make_async_copy(slot(first, k), obuf.at[j], sem_in.at[j]).start()

        each(cap, load)

    for i, (part, first_part, first, sign) in enumerate(specs):

        def stage(k, u, i=i, part=part, first_part=first_part, first=first):
            j = i * cap + k
            at = lead_ref[start + j]

            @pl.when(at >= 0)
            def _():
                pltpu.make_async_copy(
                    parts[part].at[:, first_part + k], pbuf.at[j], sem_part.at[j]
                ).wait()
                tmp[u][...] = widen(pbuf[j])

            @pl.when(at == j)
            def _():
                pltpu.make_async_copy(slot(first, k), obuf.at[j], sem_in.at[j]).wait()

        def process(k, u, i=i, sign=sign):
            j = i * cap + k
            at = lead_ref[start + j]

            def term(c):
                value = tmp[u][pl.ds(c, dofs, stride=coeffs), :]
                return value if sign > 0 else -value

            @pl.when(at == j)
            def _():
                for c in range(coeffs):
                    acc[j, c] = obuf[j, c].astype(F32) + term(c)

            @pl.when((at >= 0) & (at < j))
            def _():
                for c in range(coeffs):
                    acc[at, c] = acc[at, c] + term(c)

        batched(cap, stage, process)

    def store(first, k, j):
        return pltpu.make_async_copy(obuf.at[j], slot(first, k), sem_out.at[j])

    for i, (_, _, first, _) in enumerate(specs):

        def finish(k, i=i, first=first):
            j = i * cap + k

            @pl.when(lead_ref[start + j] == j)
            def _():
                obuf[j] = acc[j].astype(BF16)
                store(first, k, j).start()

        each(cap, finish)
    for i, (_, _, first, _) in enumerate(specs):

        def drain(k, i=i, first=first):
            j = i * cap + k

            @pl.when(lead_ref[start + j] == j)
            def _():
                store(first, k, j).wait()

        each(cap, drain)


def add_pairs(cap, specs, start, tab, lead, parts, deps, out):
    n = cap * len(specs)
    coeffs, dofs, lanes = out.shape[1], out.shape[3], out.shape[4]
    peers, rows = parts[0].shape[0], parts[0].shape[2]
    return pl.pallas_call(
        functools.partial(add_kernel, cap, specs, start, len(deps)),
        out_shape=jax.ShapeDtypeStruct(out.shape, out.dtype),
        in_specs=[SMEM, SMEM] + [ANY] * (len(parts) + len(deps) + 1),
        out_specs=ANY,
        scratch_shapes=[
            pltpu.VMEM((n, coeffs, dofs, lanes), F32),
            pltpu.VMEM((n, coeffs, dofs, lanes), BF16),
            pltpu.VMEM((n, peers, rows, lanes), BF16),
        ]
        + [pltpu.SemaphoreType.DMA((n,))] * 3
        + [pltpu.VMEM((coeffs * dofs, lanes), F32)] * unrolled(cap),
        input_output_aliases={2 + len(parts) + len(deps): 0},
        compiler_params=memory(16),
        name="add_pairs",
    )(tab, lead, *parts, *deps, out)


def stiffness_kernel(n_extra, matrix_ref, x_ref, *refs):
    out_ref = refs[n_extra]
    matrix = matrix_ref[0]
    lanes = x_ref.shape[4]
    for s in range(x_ref.shape[0]):
        rhs = jnp.concatenate([x_ref[s, 0, 0], x_ref[s, 0, 1]], axis=1)
        value = jnp.dot(matrix, rhs, preferred_element_type=F32).astype(BF16)
        for p in range(2):
            out_ref[s, 0, p] = value[:, p * lanes : (p + 1) * lanes]


def stiffness_product(stiffness, paired, first, count, out, deps):
    size = stiffness.shape[1]
    sectors, lanes = paired.shape[0], paired.shape[4]
    tile = size // 2
    extra = deps if out is None else [out] + deps
    return pl.pallas_call(
        functools.partial(stiffness_kernel, len(extra)),
        grid=(count, size // tile),
        in_specs=[
            pl.BlockSpec((1, tile, size), lambda i, j: (first + i, j, 0)),
            pl.BlockSpec((sectors, 1, 2, size, lanes), lambda i, j: (0, first + i, 0, 0, 0)),
        ]
        + [ANY] * len(extra),
        out_specs=pl.BlockSpec(
            (sectors, 1, 2, tile, lanes), lambda i, j: (0, first + i, 0, j, 0)
        ),
        out_shape=jax.ShapeDtypeStruct(paired.shape, BF16),
        input_output_aliases={} if out is None else {2: 0},
        cost_estimate=pl.CostEstimate(
            flops=4 * count * size * size * sectors * lanes,
            bytes_accessed=2 * count * size * (size + 4 * sectors * lanes),
            transcendentals=0,
        ),
        name="stiffness_product",
    )(stiffness, paired, *extra)


def on_device(displacement, stiffness, contact_limit, pair_list, pair_count):
    sec_count = lax.axis_size("sec")
    harm_count = lax.axis_size("harm")
    sectors, coeffs, blocks, dofs, lanes = displacement.shape
    harmonics = stiffness.shape[0]
    cap = pair_list.shape[0] // sec_count // 3
    slots = 3 * cap
    rows = coeffs * dofs // harm_count
    fwd, inv = tables(NT, coeffs * harm_count)
    share = (harm_count, rows, lanes)
    wire = jax.ShapeDtypeStruct((harm_count, cap, rows, lanes), BF16)
    double = jax.ShapeDtypeStruct((harm_count, 2 * cap, rows, lanes), BF16)
    sec = lax.axis_index("sec").astype(jnp.int32).reshape(1)
    listing = (sec, pair_list.T, pair_count)
    raw_slot = (coeffs, dofs, lanes)
    flats = [pltpu.VMEM((coeffs * dofs, lanes), F32)] * unrolled(cap)

    partner, owner = 0, 3 * slots
    calls = (
        (partner + cap, partner + 2 * cap, owner + cap),
        (partner, owner, owner + 2 * cap),
    )

    to_next, to_prev, own = pl.pallas_call(
        functools.partial(send_kernel, cap, sectors, sec_count),
        out_shape=[wire, wire, jax.ShapeDtypeStruct((4 * slots,), jnp.int32)],
        in_specs=[SMEM, SMEM, SMEM, ANY],
        out_specs=[ANY, ANY, SMEM],
        scratch_shapes=[
            pltpu.VMEM((2 * cap,) + raw_slot, BF16),
            pltpu.VMEM((2 * cap,) + share, BF16),
            pltpu.SemaphoreType.DMA((2 * cap,)),
            pltpu.SemaphoreType.DMA((2 * cap,)),
        ]
        + flats,
        name="send",
    )(*listing, displacement)

    forward = [(i, (i + 1) % sec_count) for i in range(sec_count)]
    backward = [((i + 1) % sec_count, i) for i in range(sec_count)]
    from_prev = lax.ppermute(to_next, "sec", forward)

    def gather(n):
        return [
            pltpu.VMEM((2 * cap,) + raw_slot, BF16),
            pltpu.VMEM((n * cap,) + share, BF16),
        ]

    diff_local = pl.pallas_call(
        functools.partial(local_kernel, cap),
        out_shape=wire,
        in_specs=[SMEM, ANY],
        out_specs=ANY,
        scratch_shapes=gather(1)
        + [pltpu.SemaphoreType.DMA((2 * cap,)), pltpu.SemaphoreType.DMA((cap,))]
        + flats,
        name="local",
    )(own, displacement)
    limit = contact_limit.reshape(-1)
    limit = jnp.concatenate([limit, 1.0 / limit])
    gathered = pl.pallas_call(
        functools.partial(partner_kernel, cap, sectors, sec_count, calls),
        out_shape=[wire] * 2
        + [jax.ShapeDtypeStruct((6 * n,), jnp.int32) for n in (slots, cap)]
        + [jax.ShapeDtypeStruct((2 * slots * contact_limit.shape[2],), F32)],
        in_specs=[SMEM] * 5 + [ANY, ANY],
        out_specs=[ANY, ANY, SMEM, SMEM, SMEM],
        scratch_shapes=gather(2)
        + [pltpu.SMEM((sectors * blocks,), jnp.int32)]
        + [pltpu.SemaphoreType.DMA((2 * cap,))] * 2
        + flats,
        name="partner",
    )(*listing, own, limit, displacement, diff_local)
    at_a, at_b, tab, lead, limits = gathered

    to_prev, from_prev, at_b = lax.optimization_barrier((to_prev, from_prev, at_b))
    from_next = lax.ppermute(to_prev, "sec", backward)


    def exchange(x):
        return lax.all_to_all(x, "harm", split_axis=0, concat_axis=0, tiled=True)

    def product(first, count, out, deps):
        return stiffness_product(stiffness, paired, first, count, out, deps)

    def friction(group, x, first, extra=()):
        n = cap * (2 if extra else 1)
        return pl.pallas_call(
            functools.partial(friction_kernel, cap, group, first, bool(extra)),
            out_shape=double if extra else wire,
            in_specs=[SMEM, VMEM, VMEM] + [ANY] * (1 + len(extra)),
            out_specs=ANY,
            scratch_shapes=[
                pltpu.VMEM((cap,) + share, BF16),
                pltpu.VMEM((n,) + share, BF16),
                pltpu.SemaphoreType.DMA((4, n)),
            ]
            + [pltpu.VMEM((cap,) + share, BF16)] * len(extra),
            compiler_params=memory(12),
            name="friction",
        )(limits, fwd, inv, x, *extra)

    paired = displacement.reshape(sectors, harmonics, 2, blocks * dofs, lanes)
    quarter = max(harmonics // 4, 1)
    third = harmonics - 2 * quarter

    local_x = exchange(diff_local)
    diff_a = pl.pallas_call(
        difference_kernel,
        out_shape=wire,
        in_specs=[VMEM, VMEM, ANY],
        out_specs=VMEM,
        compiler_params=memory(8),
        name="difference",
    )(from_prev, at_a, local_x)
    a_x = exchange(diff_a)
    out = product(0, quarter, None, [diff_a])
    middle = friction(1, a_x, 0, (from_next, at_b))
    mixed = exchange(middle)
    out = product(quarter, third, out, [middle])
    force_local = friction(0, local_x, 0)
    ret_a = lax.ppermute(mixed[:, :cap], "sec", backward)
    force_b = friction(2, mixed, cap)
    back_b = exchange(force_b)
    out = product(quarter + third, quarter, out, [force_b])
    back_b, force_local, out = lax.optimization_barrier((back_b, force_local, out))
    ret_b = lax.ppermute(back_b, "sec", forward)
    back_local = exchange(force_local)

    out = out.reshape(displacement.shape)
    out = add_pairs(
        cap,
        ((0, 0, calls[0][0], -1), (1, 0, calls[0][1], -1), (2, 0, calls[0][2], 1)),
        0,
        tab,
        lead,
        [mixed, back_b, ret_a],
        [],
        out,
    )
    return add_pairs(
        cap,
        ((0, 0, calls[1][0], -1), (0, 0, calls[1][1], 1), (1, 0, calls[1][2], 1)),
        3 * cap,
        tab,
        lead,
        [back_local, ret_b],
        [],
        out,
    )


def solution(mesh):
    in_specs = (
        P("sec", "harm", None, None, None),
        P("harm", None, None),
        P("sec", None, "harm"),
        P(),
        P(),
    )
    out_specs = P("sec", "harm", None, None, None)

    return jax.shard_map(
        on_device, mesh=mesh, in_specs=in_specs, out_specs=out_specs, check_vma=False
    )
```

```python
import functools
import math

import jax
import jax.numpy as jnp
import numpy as np
from jax import lax
from jax.experimental import pallas as pl
from jax.experimental.pallas import tpu as pltpu
from jax.sharding import PartitionSpec as P


NT = 128
ANY = pl.BlockSpec(memory_space=pl.ANY)
SMEM = pl.BlockSpec(memory_space=pltpu.SMEM)
VMEM = pl.BlockSpec(memory_space=pltpu.VMEM)
F32 = jnp.float32
BF16 = jnp.bfloat16


def tables(sample_count, coeff_count):
    n_index = np.arange(sample_count)[:, None]
    c_index = np.arange(coeff_count)[None, :]
    phases = 2.0 * math.pi * ((c_index // 2 + 1) * n_index % sample_count) / sample_count
    wave = np.where(c_index % 2 == 0, np.cos(phases), np.sin(phases)).astype(np.float32)
    return jnp.asarray(wave, BF16), jnp.asarray(wave.T * np.float32(2.0 / sample_count), BF16)


def memory(mib):
    return pltpu.CompilerParams(vmem_limit_bytes=mib << 20)


def scan_rows(cap, sectors_here, sec_count, list_ref, count_ref, device, emit):
    slots = 3 * cap
    total = sectors_here * sec_count
    used = count_ref[device]

    def row(r, ranks):
        at = device * slots + r
        owner, partner, block = list_ref[0, at], list_ref[1, at], list_ref[2, at]
        local = partner - device * sectors_here
        here = (local >= 0) & (local < sectors_here)
        following = jnp.where(owner + 1 == total, 0, owner + 1)
        group = jnp.where(here, 0, jnp.where(partner == following, 1, 2))
        valid = r < used
        rank = jnp.where(group == 0, ranks[0], jnp.where(group == 1, ranks[1], ranks[2]))

        @pl.when(valid & (rank < cap))
        def _():
            emit(group, rank, owner, partner, block)

        return tuple(
            ranks[g] + jnp.where(valid & (group == g), 1, 0).astype(jnp.int32) for g in range(3)
        )

    lax.fori_loop(0, slots, row, (jnp.int32(0),) * 3)


def widen(value):
    return value.astype(F32).reshape(-1, value.shape[-1])


def unrolled(count):
    return next(u for u in (3, 2, 1) if count % u == 0)


def each(count, body):
    def step(k, carry):
        body(k)
        return carry

    lax.fori_loop(0, count, step, 0)


def batched(count, stage, process):
    width = unrolled(count)

    def step(i, carry):
        for u in range(width):
            stage(i * width + u, u)
        for u in range(width):
            process(i * width + u, u)
        return carry

    lax.fori_loop(0, count // width, step, 0)


def swap_rows(tmp_ref, buf, coeffs, dofs):
    peers, rows = buf.shape[0], buf.shape[1]
    share = rows // coeffs
    for h in range(peers):
        buf[h] = jnp.concatenate(
            [tmp_ref[pl.ds(h * share + d, coeffs, stride=dofs), :] for d in range(share)], axis=0
        ).astype(BF16)


def send_kernel(cap, sectors_here, sec_count, sec_ref, list_ref, count_ref, disp_ref,
                next_ref, tab_ref, raw, buf, sem, sem_out, *tmp):
    slots = 3 * cap
    me = sec_ref[0]
    base = me * sectors_here
    scan = functools.partial(scan_rows, cap, sectors_here, sec_count, list_ref, count_ref)

    def clear(i):
        tab_ref[i] = 0

    each(6 * slots, clear)

    def own(group, rank, owner, partner, block):
        at = group * cap + rank
        tab_ref[3 * slots + at] = owner - base
        tab_ref[4 * slots + at] = block
        tab_ref[5 * slots + at] = 1

        @pl.when(group == 0)
        def _():
            tab_ref[at] = partner - base
            tab_ref[slots + at] = block
            tab_ref[2 * slots + at] = 1

    scan(me, own)

    def copy(k):
        at = 3 * slots + cap + k
        source = disp_ref.at[tab_ref[at], :, tab_ref[slots + at]]
        return pltpu.make_async_copy(source, raw.at[k], sem.at[k])

    each(cap, lambda k: copy(k).start())

    def incoming(wanted):
        def emit(group, rank, owner, partner, block):
            @pl.when(group == wanted)
            def _():
                at = wanted * cap + rank
                tab_ref[at] = partner - base
                tab_ref[slots + at] = block
                tab_ref[2 * slots + at] = 1

        return emit

    scan(jnp.where(me == 0, sec_count - 1, me - 1), incoming(1))
    scan(jnp.where(me == sec_count - 1, 0, me + 1), incoming(2))
    coeffs, dofs = raw.shape[1], raw.shape[2]

    def out(k):
        return pltpu.make_async_copy(buf.at[k], next_ref.at[:, k], sem_out.at[k])

    def stage(k, u):
        copy(k).wait()
        tmp[u][...] = widen(raw[k])

    def process(k, u):
        swap_rows(tmp[u], buf.at[k], coeffs, dofs)
        out(k).start()

    batched(cap, stage, process)
    each(cap, lambda k: out(k).wait())


def find_leaders(cap, blocks, sectors_here, calls, tab_ref, lead_ref, seen):
    slots = 3 * cap
    start = 0
    for firsts in calls:

        def clear(i):
            seen[i] = -1

        each(sectors_here * blocks, clear)
        for i, first in enumerate(firsts):

            def mark(k, i=i, first=first, start=start):
                at = first + k
                j = i * cap + k
                key = tab_ref[at] * blocks + tab_ref[slots + at]
                live = tab_ref[2 * slots + at] > 0
                found = jnp.where(seen[key] < 0, j, seen[key])
                lead_ref[start + j] = jnp.where(live, found, -1)
                seen[key] = jnp.where(live, found, seen[key])

            each(cap, mark)
        start += cap * len(firsts)


def local_kernel(cap, tab_ref, disp_ref, diff_ref, raw, buf, sem, sem_out, *tmp):
    slots = 3 * cap

    def copy(sec_at, blk_at, j):
        source = disp_ref.at[tab_ref[sec_at], :, tab_ref[blk_at]]
        return pltpu.make_async_copy(source, raw.at[j], sem.at[j])

    def owner(k):
        return copy(3 * slots + k, 4 * slots + k, k)

    def partner(k):
        return copy(k, slots + k, cap + k)

    def start(k):
        owner(k).start()
        partner(k).start()

    each(cap, start)
    coeffs, dofs = raw.shape[1], raw.shape[2]

    def out(k):
        return pltpu.make_async_copy(buf.at[k], diff_ref.at[:, k], sem_out.at[k])

    def stage(k, u):
        owner(k).wait()
        partner(k).wait()
        tmp[u][...] = widen(raw[k]) - widen(raw[cap + k])

    def process(k, u):
        swap_rows(tmp[u], buf.at[k], coeffs, dofs)
        out(k).start()

    batched(cap, stage, process)
    each(cap, lambda k: out(k).wait())


def partner_kernel(cap, sectors_here, calls, tab_ref, lim_ref, disp_ref, dep_ref,
                   a_ref, prev_ref, b_ref, lead_ref, pick_ref, raw, buf, seen, sem, sem_out,
                   *tmp):
    slots = 3 * cap
    groups = ((cap, a_ref), (3 * slots + 2 * cap, prev_ref), (2 * cap, b_ref))

    def copy(g, k):
        at = groups[g][0] + k
        source = disp_ref.at[tab_ref[at], :, tab_ref[slots + at]]
        return pltpu.make_async_copy(source, raw.at[g * cap + k], sem.at[g * cap + k])

    for g in range(3):
        each(cap, lambda k, g=g: copy(g, k).start())
    blocks = disp_ref.shape[2]
    find_leaders(cap, blocks, sectors_here, calls, tab_ref, lead_ref, seen)
    total = lim_ref.shape[0] // 2
    share = total // (sectors_here * blocks)

    def pick(p):
        at = (tab_ref[p] * blocks + tab_ref[slots + p]) * share
        for d in range(share):
            pick_ref[p * share + d] = lim_ref[at + d]
            pick_ref[(slots + p) * share + d] = lim_ref[total + at + d]

    each(slots, pick)
    coeffs, dofs = raw.shape[1], raw.shape[2]

    def out(g, k):
        j = g * cap + k
        return pltpu.make_async_copy(buf.at[j], groups[g][1].at[:, k], sem_out.at[j])

    for g in range(3):

        def stage(k, u, g=g):
            copy(g, k).wait()
            tmp[u][...] = widen(raw[g * cap + k])

        def process(k, u, g=g):
            swap_rows(tmp[u], buf.at[g * cap + k], coeffs, dofs)
            out(g, k).start()

        batched(cap, stage, process)
    for g in range(3):
        each(cap, lambda k, g=g: out(g, k).wait())


def friction_pair(base, rec_base, lim_ref, fwd_ref, inv_ref, x_ref, o_ref):
    peers, rows, lanes = x_ref.shape
    coeffs = fwd_ref.shape[1] // peers
    dofs = rows // coeffs
    parts = [x_ref[h].astype(F32) for h in range(peers)]
    columns = jnp.concatenate(
        [
            jnp.concatenate([x[d * coeffs : (d + 1) * coeffs] for x in parts], axis=0)
            for d in range(dofs)
        ],
        axis=1,
    ).astype(BF16)
    wave = jnp.dot(fwd_ref[...], columns, preferred_element_type=F32)
    force = jnp.concatenate(
        [
            lim_ref[base + d]
            * jnp.tanh(wave[:, d * lanes : (d + 1) * lanes] * lim_ref[rec_base + d])
            for d in range(dofs)
        ],
        axis=1,
    ).astype(BF16)
    back = jnp.dot(inv_ref[...], force, preferred_element_type=F32)
    for h in range(peers):
        o_ref[h] = jnp.concatenate(
            [
                back[h * coeffs : (h + 1) * coeffs, d * lanes : (d + 1) * lanes]
                for d in range(dofs)
            ],
            axis=0,
        ).astype(BF16)


def difference_kernel(x_ref, y_ref, *refs):
    o_ref = refs[-1]

    def subtract(h):
        o_ref[h] = (x_ref[h].astype(F32) - y_ref[h].astype(F32)).astype(BF16)

    each(x_ref.shape[0], subtract)


def friction_kernel(cap, group, first, with_difference, lim_ref, fwd_ref, inv_ref, x_ref, *refs):
    slots = 3 * cap
    if with_difference:
        y_ref, z_ref, o_ref, o_buf, sem = refs
    else:
        o_ref, o_buf, sem = refs
    dofs = x_ref.shape[2] * x_ref.shape[0] // fwd_ref.shape[1]

    def out(k):
        return pltpu.make_async_copy(o_buf.at[k], o_ref.at[:, k], sem.at[k])

    if with_difference:

        def subtract(k):
            for h in range(x_ref.shape[0]):
                value = y_ref[h, k].astype(F32) - z_ref[h, k].astype(F32)
                o_buf[cap + k, h] = value.astype(BF16)
            out(cap + k).start()

        each(cap, subtract)

    def process(k, u):
        base = (group * cap + k) * dofs
        rec_base = base + slots * dofs
        friction_pair(base, rec_base, lim_ref, fwd_ref, inv_ref, x_ref.at[:, first + k], o_buf.at[k])
        out(k).start()

    batched(cap, lambda k, u: None, process)
    each(o_ref.shape[1], lambda k: out(k).wait())


def add_kernel(cap, specs, start, n_deps, tab_ref, lead_ref, *refs):
    n_parts = len({spec[0] for spec in specs})
    parts = refs[:n_parts]
    refs = refs[n_parts + n_deps + 1 :]
    out_ref, acc, obuf, sem_in, sem_out = refs[:5]
    tmp = refs[5:]
    slots = 3 * cap
    coeffs, dofs = acc.shape[1], acc.shape[2]

    def slot(first, k):
        return out_ref.at[tab_ref[first + k], :, tab_ref[slots + first + k]]

    for i, (_, _, first, _) in enumerate(specs):

        def load(k, i=i, first=first):
            j = i * cap + k

            @pl.when(lead_ref[start + j] == j)
            def _():
                pltpu.make_async_copy(slot(first, k), obuf.at[j], sem_in.at[j]).start()

        each(cap, load)

    for i, (part, first_part, first, sign) in enumerate(specs):

        def stage(k, u, i=i, ref=parts[part], first_part=first_part, first=first):
            j = i * cap + k
            rows = ref.shape[2]
            for h in range(ref.shape[0]):
                tmp[u][pl.ds(h * rows, rows), :] = ref[h, first_part + k].astype(F32)

            @pl.when(lead_ref[start + j] == j)
            def _():
                pltpu.make_async_copy(slot(first, k), obuf.at[j], sem_in.at[j]).wait()

        def process(k, u, i=i, sign=sign):
            j = i * cap + k
            at = lead_ref[start + j]

            def term(c):
                value = tmp[u][pl.ds(c, dofs, stride=coeffs), :]
                return value if sign > 0 else -value

            @pl.when(at == j)
            def _():
                for c in range(coeffs):
                    acc[j, c] = obuf[j, c].astype(F32) + term(c)

            @pl.when((at >= 0) & (at < j))
            def _():
                for c in range(coeffs):
                    acc[at, c] = acc[at, c] + term(c)

        batched(cap, stage, process)

    def store(first, k, j):
        return pltpu.make_async_copy(obuf.at[j], slot(first, k), sem_out.at[j])

    for i, (_, _, first, _) in enumerate(specs):

        def finish(k, i=i, first=first):
            j = i * cap + k

            @pl.when(lead_ref[start + j] == j)
            def _():
                obuf[j] = acc[j].astype(BF16)
                store(first, k, j).start()

        each(cap, finish)
    for i, (_, _, first, _) in enumerate(specs):

        def drain(k, i=i, first=first):
            j = i * cap + k

            @pl.when(lead_ref[start + j] == j)
            def _():
                store(first, k, j).wait()

        each(cap, drain)


def add_pairs(cap, specs, start, tab, lead, parts, deps, out):
    n = cap * len(specs)
    coeffs, dofs, lanes = out.shape[1], out.shape[3], out.shape[4]
    return pl.pallas_call(
        functools.partial(add_kernel, cap, specs, start, len(deps)),
        out_shape=jax.ShapeDtypeStruct(out.shape, out.dtype),
        in_specs=[SMEM, SMEM] + [VMEM] * len(parts) + [ANY] * (len(deps) + 1),
        out_specs=ANY,
        scratch_shapes=[
            pltpu.VMEM((n, coeffs, dofs, lanes), F32),
            pltpu.VMEM((n, coeffs, dofs, lanes), BF16),
        ]
        + [pltpu.SemaphoreType.DMA((n,))] * 2
        + [pltpu.VMEM((coeffs * dofs, lanes), F32)] * unrolled(cap),
        input_output_aliases={2 + len(parts) + len(deps): 0},
        compiler_params=memory(16),
        name="add_pairs",
    )(tab, lead, *parts, *deps, out)


def stiffness_kernel(n_extra, matrix_ref, x_ref, *refs):
    out_ref = refs[n_extra]
    matrix = matrix_ref[0]
    lanes = x_ref.shape[4]
    for s in range(x_ref.shape[0]):
        rhs = jnp.concatenate([x_ref[s, 0, 0], x_ref[s, 0, 1]], axis=1)
        value = jnp.dot(matrix, rhs, preferred_element_type=F32).astype(BF16)
        for p in range(2):
            out_ref[s, 0, p] = value[:, p * lanes : (p + 1) * lanes]


def stiffness_product(stiffness, paired, first, count, out, deps):
    size = stiffness.shape[1]
    sectors, lanes = paired.shape[0], paired.shape[4]
    tile = size // 2
    extra = deps if out is None else [out] + deps
    return pl.pallas_call(
        functools.partial(stiffness_kernel, len(extra)),
        grid=(count, size // tile),
        in_specs=[
            pl.BlockSpec((1, tile, size), lambda i, j: (first + i, j, 0)),
            pl.BlockSpec((sectors, 1, 2, size, lanes), lambda i, j: (0, first + i, 0, 0, 0)),
        ]
        + [ANY] * len(extra),
        out_specs=pl.BlockSpec(
            (sectors, 1, 2, tile, lanes), lambda i, j: (0, first + i, 0, j, 0)
        ),
        out_shape=jax.ShapeDtypeStruct(paired.shape, BF16),
        input_output_aliases={} if out is None else {2: 0},
        cost_estimate=pl.CostEstimate(
            flops=4 * count * size * size * sectors * lanes,
            bytes_accessed=2 * count * size * (size + 4 * sectors * lanes),
            transcendentals=0,
        ),
        name="stiffness_product",
    )(stiffness, paired, *extra)


def on_device(displacement, stiffness, contact_limit, pair_list, pair_count):
    sec_count = lax.axis_size("sec")
    harm_count = lax.axis_size("harm")
    sectors, coeffs, blocks, dofs, lanes = displacement.shape
    harmonics = stiffness.shape[0]
    cap = pair_list.shape[0] // sec_count // 3
    slots = 3 * cap
    rows = coeffs * dofs // harm_count
    fwd, inv = tables(NT, coeffs * harm_count)
    share = (harm_count, rows, lanes)
    wire = jax.ShapeDtypeStruct((harm_count, cap, rows, lanes), BF16)
    double = jax.ShapeDtypeStruct((harm_count, 2 * cap, rows, lanes), BF16)
    sec = lax.axis_index("sec").astype(jnp.int32).reshape(1)
    raw_slot = (coeffs, dofs, lanes)
    flats = [pltpu.VMEM((coeffs * dofs, lanes), F32)] * unrolled(cap)

    partner, owner = 0, 3 * slots
    calls = (
        (partner + cap, partner + 2 * cap, owner + cap),
        (partner, owner, owner + 2 * cap),
    )

    def gather(n_in, n_out):
        return [
            pltpu.VMEM((n_in * cap,) + raw_slot, BF16),
            pltpu.VMEM((n_out * cap,) + share, BF16),
        ]

    def semaphores(n_in, n_out):
        return [pltpu.SemaphoreType.DMA((n * cap,)) for n in (n_in, n_out)]

    to_next, tab = pl.pallas_call(
        functools.partial(send_kernel, cap, sectors, sec_count),
        out_shape=[wire, jax.ShapeDtypeStruct((6 * slots,), jnp.int32)],
        in_specs=[SMEM, SMEM, SMEM, ANY],
        out_specs=[ANY, SMEM],
        scratch_shapes=gather(1, 1) + semaphores(1, 1) + flats,
        name="send",
    )(sec, pair_list.T, pair_count, displacement)

    forward = [(i, (i + 1) % sec_count) for i in range(sec_count)]
    backward = [((i + 1) % sec_count, i) for i in range(sec_count)]
    from_prev = lax.ppermute(to_next, "sec", forward)

    diff_local = pl.pallas_call(
        functools.partial(local_kernel, cap),
        out_shape=wire,
        in_specs=[SMEM, ANY],
        out_specs=ANY,
        scratch_shapes=gather(2, 1) + semaphores(2, 1) + flats,
        name="local",
    )(tab, displacement)
    limit = contact_limit.reshape(-1)
    limit = jnp.concatenate([limit, 1.0 / limit])
    at_a, to_prev, at_b, lead, limits = pl.pallas_call(
        functools.partial(partner_kernel, cap, sectors, calls),
        out_shape=[wire] * 3
        + [jax.ShapeDtypeStruct((6 * cap,), jnp.int32)]
        + [jax.ShapeDtypeStruct((2 * slots * contact_limit.shape[2],), F32)],
        in_specs=[SMEM, SMEM, ANY, ANY],
        out_specs=[ANY, ANY, ANY, SMEM, SMEM],
        scratch_shapes=gather(3, 3)
        + [pltpu.SMEM((sectors * blocks,), jnp.int32)]
        + semaphores(3, 3)
        + flats,
        name="partner",
    )(tab, limit, displacement, diff_local)
    to_prev, from_prev = lax.optimization_barrier((to_prev, from_prev))
    from_next = lax.ppermute(to_prev, "sec", backward)

    def exchange(x):
        return lax.all_to_all(x, "harm", split_axis=0, concat_axis=0, tiled=True)

    def product(first, count, out, deps):
        return stiffness_product(stiffness, paired, first, count, out, deps)

    def friction(group, x, first, extra=()):
        n = cap * (2 if extra else 1)
        return pl.pallas_call(
            functools.partial(friction_kernel, cap, group, first, bool(extra)),
            out_shape=double if extra else wire,
            in_specs=[SMEM] + [VMEM] * (3 + len(extra)),
            out_specs=ANY,
            scratch_shapes=[pltpu.VMEM((n,) + share, BF16), pltpu.SemaphoreType.DMA((n,))],
            compiler_params=memory(12),
            name="friction",
        )(limits, fwd, inv, x, *extra)

    paired = displacement.reshape(sectors, harmonics, 2, blocks * dofs, lanes)
    quarter = max(harmonics // 4, 1)
    third = harmonics - 2 * quarter

    local_x = exchange(diff_local)
    diff_a = pl.pallas_call(
        difference_kernel,
        out_shape=wire,
        in_specs=[VMEM, VMEM, ANY],
        out_specs=VMEM,
        compiler_params=memory(8),
        name="difference",
    )(from_prev, at_a, local_x)
    a_x = exchange(diff_a)
    out = product(0, quarter, None, [diff_a])
    middle = friction(1, a_x, 0, (from_next, at_b))
    mixed = exchange(middle)
    out = product(quarter, third, out, [middle])
    force_local = friction(0, local_x, 0)
    ret_a = lax.ppermute(mixed[:, :cap], "sec", backward)
    force_b = friction(2, mixed, cap)
    back_b = exchange(force_b)
    out = product(quarter + third, quarter, out, [force_b])
    back_b, force_local, out = lax.optimization_barrier((back_b, force_local, out))
    ret_b = lax.ppermute(back_b, "sec", forward)
    back_local = exchange(force_local)

    out = out.reshape(displacement.shape)
    out = add_pairs(
        cap,
        ((0, 0, calls[0][0], -1), (1, 0, calls[0][1], -1), (2, 0, calls[0][2], 1)),
        0,
        tab,
        lead,
        [mixed, back_b, ret_a],
        [],
        out,
    )
    return add_pairs(
        cap,
        ((0, 0, calls[1][0], -1), (0, 0, calls[1][1], 1), (1, 0, calls[1][2], 1)),
        3 * cap,
        tab,
        lead,
        [back_local, ret_b],
        [],
        out,
    )


def solution(mesh):
    in_specs = (
        P("sec", "harm", None, None, None),
        P("harm", None, None),
        P("sec", None, "harm"),
        P(),
        P(),
    )
    out_specs = P("sec", "harm", None, None, None)

    return jax.shard_map(
        on_device, mesh=mesh, in_specs=in_specs, out_specs=out_specs, check_vma=False
    )
```
